32 devices in a mesh: dp: 2 (over x), cols: 16 (over z, y, core).
Axes of the slice: x: 2, y: 2, z: 4, core: 2. Of those that a mesh axis runs over, the one named last changes fastest.
Arguments:
- tokens: bfloat16 [512, 4096], P(('dp', 'cols')), may hold values from -6 to 6
- cotangent: bfloat16 [512, 4096], P(('dp', 'cols')), may hold values from -6 to 6
- block_weights: bfloat16 [4096, 128, 128], P('cols'), may hold values from -0.15625 to 0.15625
- slot_block: int32 [4096], P('cols'), may hold values from 0 to 31
- slot_target: int32 [4096], P('cols'), may hold values from 0 to 23, as said below
- counts: int32 [16], P('cols'), may hold values from 171 to 256, as said below
Outputs:
- input_grad: bfloat16 [512, 4096], P(('dp', 'cols'))
- weight_grad: bfloat16 [4096, 128, 128], P('cols', 'dp')
The draws below stay inside these ranges and needn't reach their ends.
Inputs may be any that keep to these rules, and one draw needn't show every extreme that they name: On each device the live slots name distinct pairs of slot_target and slot_block; slot_target // 8 gives the matrix (0 gate, 1 up, 2 down). `counts`: some device has all 256 slots live.
All inputs are finite; a program needn't handle non-finite values.
Results may differ from the reference program's by a relative error of at most 0.018.
Values may be sent and summed in bfloat16 or wider, within the bound.
A program may use at most 192 MiB of HBM per device.

```python
import jax
import jax.numpy as jnp
from jax import lax

D = 4096
BLK = 128
NDB = 32
CPD = 8
SLOTS = 256
TOKENS = 512
N_DP = 2
N_COLS = 16


def pattern(key):
    base_key = jax.random.fold_in(key, 17)
    device_keys = jax.random.split(base_key, N_COLS)
    pair_total = 3 * CPD * NDB
    chosen = jax.vmap(lambda device_key: jax.random.permutation(device_key, pair_total)[:SLOTS])(device_keys)
    return chosen.reshape(-1).astype(jnp.int32)


def draw_slot_block(key, part):
    return (pattern(key) % NDB).astype(jnp.int32)


def draw_slot_target(key, part):
    return (pattern(key) // NDB).astype(jnp.int32)


def draw_counts(key, part):
    first_key, second_key = jax.random.split(jax.random.fold_in(key, 29))
    totals = jax.random.randint(first_key, (N_COLS,), SLOTS - SLOTS // 3, SLOTS + 1)
    device_pick = jax.random.randint(second_key, (), 0, N_COLS)
    return totals.at[device_pick].set(SLOTS).astype(jnp.int32)


def block_levels(rng, dims, cuts, low, top_value):
    loudness, own = 1.0, jax.random.fold_in(rng, 6)
    for axis_at, parts in cuts:
        steps = jnp.exp(jax.random.uniform(jax.random.fold_in(own, axis_at), (parts,), jnp.float32, low / len(cuts), top_value / len(cuts)))
        loudness = loudness * jnp.repeat(steps, dims[axis_at] // parts).reshape([-1 if axis == axis_at else 1 for axis in range(len(dims))])
    return loudness


def gaussian(own_key, extent, deviation, limit, pieces=(), kind=jnp.bfloat16):
    drawn = deviation * jax.random.normal(own_key, extent, jnp.float32)
    if pieces:
        drawn = drawn * block_levels(own_key, extent, pieces, -0.22, 0.18)
    return jnp.clip(drawn, -limit, limit).astype(kind)


def setup_inputs(seed: int = 0) -> dict:
    streams_of = jax.random.split(jax.random.key(seed), 7)
    tokens = gaussian(streams_of[0], (TOKENS, D), 1.0, 6.0, ((0, 32),))
    cotangent = gaussian(streams_of[1], (TOKENS, D), 1.0, 6.0, ((0, 32),))
    block_weights = gaussian(streams_of[2], (N_COLS * SLOTS, BLK, BLK), (BLK * SLOTS // (3 * CPD)) ** -0.5, 0.15625, ((0, 16),))
    slot_block = draw_slot_block(jax.random.fold_in(streams_of[6], 71), 0)
    slot_target = draw_slot_target(jax.random.fold_in(streams_of[6], 71), 0)
    counts = draw_counts(jax.random.fold_in(streams_of[6], 71), 0)
    return {"tokens": tokens, "cotangent": cotangent, "block_weights": block_weights, "slot_block": slot_block, "slot_target": slot_target, "counts": counts}


def local_pass(tokens_rows, cotangent_rows, weights, slot_blocks, slot_targets, live_count):
    row_count = tokens_rows.shape[0]
    slot_total = weights.shape[0]
    block_width = weights.shape[1]
    block_count = tokens_rows.shape[1] // block_width
    columns = CPD
    live_slot = jnp.arange(slot_total) < live_count
    slot_kind = slot_targets // columns
    places = slot_targets % columns
    select_up = jax.nn.one_hot(slot_targets, 2 * columns, dtype=jnp.float32) * (live_slot & (slot_kind < 2))[:, None].astype(jnp.float32)
    select_down = jax.nn.one_hot(places, columns, dtype=jnp.float32) * (live_slot & (slot_kind == 2))[:, None].astype(jnp.float32)
    block_select = jax.nn.one_hot(slot_blocks, block_count, dtype=jnp.float32)
    wide_weights = weights.astype(jnp.float32)
    tokens_slots = jnp.take(tokens_rows.reshape(row_count, block_count, block_width), slot_blocks, axis=1).astype(jnp.float32)
    cot_slots = jnp.take(cotangent_rows.reshape(row_count, block_count, block_width), slot_blocks, axis=1).astype(jnp.float32)
    products = jnp.einsum('rsk,skj->rsj', tokens_slots, wide_weights)
    gate_up = jnp.einsum('rsj,sc->rcj', products, select_up)
    gate_pre = gate_up[:, :columns]
    up_pre = gate_up[:, columns:]
    sigmoid_gate = jax.nn.sigmoid(gate_pre)
    silu_gate = gate_pre * sigmoid_gate
    hidden = (silu_gate * up_pre).astype(jnp.bfloat16)
    back_products = jnp.einsum('rsj,skj->rsk', cot_slots, wide_weights)
    hidden_grad = jnp.einsum('rsk,sc->rck', back_products, select_down)
    gate_grad = (hidden_grad * up_pre * sigmoid_gate * (1.0 + gate_pre * (1.0 - sigmoid_gate))).astype(jnp.bfloat16)
    up_grad = (hidden_grad * silu_gate).astype(jnp.bfloat16)
    pre_grad = jnp.concatenate([gate_grad, up_grad], axis=1).astype(jnp.float32)
    slot_grad = jnp.einsum('rck,sc->rsk', pre_grad, select_up)
    slot_hidden = jnp.einsum('rck,sc->rsk', hidden.astype(jnp.float32), select_down)
    weight_terms = jnp.einsum('rsk,rsj->skj', tokens_slots, slot_grad) + jnp.einsum('rsk,rsj->skj', slot_hidden, cot_slots)
    input_slots = jnp.einsum('rsj,skj->rsk', slot_grad, wide_weights)
    input_terms = jnp.einsum('rsk,sb->rbk', input_slots, block_select).reshape(row_count, block_count * block_width)
    return weight_terms, input_terms


def reference(tokens, cotangent, block_weights, slot_block, slot_target, counts):
    row_group = tokens.shape[0] // N_DP
    weights = block_weights.reshape(N_COLS, SLOTS, BLK, BLK)
    blocks_table = slot_block.reshape(N_COLS, SLOTS)
    targets_table = slot_target.reshape(N_COLS, SLOTS)
    grad_total = jnp.zeros((N_COLS, SLOTS, BLK, BLK), jnp.float32)
    input_parts = []
    for group_index in range(N_DP):
        tokens_rows = tokens[group_index * row_group:(group_index + 1) * row_group]
        cot_rows = cotangent[group_index * row_group:(group_index + 1) * row_group]

        def device_step(carry, device_items):
            weight_one, block_one, target_one, count_one = device_items
            weight_terms, input_terms = local_pass(tokens_rows, cot_rows, weight_one, block_one, target_one, count_one)
            return carry + input_terms, weight_terms

        start_sum = jnp.zeros((row_group, tokens.shape[1]), jnp.float32)
        input_sum, weight_parts = lax.scan(device_step, start_sum, (weights, blocks_table, targets_table, counts))
        rounded = lax.optimization_barrier(weight_parts.astype(jnp.bfloat16))
        grad_total = grad_total + rounded.astype(jnp.float32)
        input_parts.append(input_sum.astype(jnp.bfloat16))
    input_grad = jnp.concatenate(input_parts, axis=0)
    weight_grad = grad_total.astype(jnp.bfloat16).reshape(N_COLS * SLOTS, BLK, BLK)
    return input_grad, weight_grad
```

```python
import functools

import jax
import jax.numpy as jnp
from jax import lax
from jax.experimental import pallas as pl
from jax.experimental.pallas import tpu as pltpu
from jax.sharding import PartitionSpec as P

SPC = 32


def block_inputs(grad_rows, weights, block_select):
    partial_rows = jnp.einsum(
        "rsj,skj->rsk", grad_rows, weights, preferred_element_type=jnp.float32
    )
    summed = jnp.einsum("rsk,sb->rbk", partial_rows, block_select)
    return summed.reshape(summed.shape[0], summed.shape[1] * summed.shape[2])


def shards(tokens, cotangent, block_weights, slot_block, slot_target, counts):
    slot_total = block_weights.shape[0]
    block_width = block_weights.shape[1]
    columns = slot_total // SPC
    features = tokens.shape[1]
    block_count = features // block_width
    tokens_all, cot_all = (
        lax.all_gather(tokens, "cols", axis=0, tiled=True),
        lax.all_gather(cotangent, "cols", axis=0, tiled=True),
    )
    row_total = tokens_all.shape[0]
    live_slot = jnp.arange(slot_total) < counts[0]
    slot_kind = slot_target // columns
    places = slot_target % columns
    up_mask = (live_slot & (slot_kind < 2))[:, None].astype(jnp.float32)
    down_mask = (live_slot & (slot_kind == 2))[:, None].astype(jnp.float32)
    select_up = jax.nn.one_hot(slot_target, 2 * columns, dtype=jnp.float32) * up_mask
    select_down = jax.nn.one_hot(places, columns, dtype=jnp.float32) * down_mask
    block_select = jax.nn.one_hot(slot_block, block_count, dtype=jnp.float32)
    tokens_slots = jnp.take(
        tokens_all.reshape(row_total, block_count, block_width), slot_block, axis=1
    )
    products = jnp.einsum(
        "rsk,skj->rsj", tokens_slots, block_weights, preferred_element_type=jnp.float32
    )
    gate_up = jnp.einsum("rsj,sc->rcj", products, select_up)
    gate_pre = gate_up[:, :columns]
    up_pre = gate_up[:, columns:]
    sigmoid_gate = jax.nn.sigmoid(gate_pre)
    silu_gate = gate_pre * sigmoid_gate
    hidden = (silu_gate * up_pre).astype(jnp.bfloat16)
    cot_slots = jnp.take(cot_all.reshape(row_total, block_count, block_width), slot_block, axis=1)
    back_products = jnp.einsum(
        "rsj,skj->rsk", cot_slots, block_weights, preferred_element_type=jnp.float32
    )
    hidden_grad = jnp.einsum("rsk,sc->rck", back_products, select_down)
    gate_grad = (
        hidden_grad * up_pre * sigmoid_gate * (1.0 + gate_pre * (1.0 - sigmoid_gate))
    ).astype(jnp.bfloat16)
    up_grad = (hidden_grad * silu_gate).astype(jnp.bfloat16)
    pre_grad = jnp.concatenate([gate_grad, up_grad], axis=1)
    slot_grad = jnp.einsum(
        "rck,sc->rsk", pre_grad, select_up.astype(jnp.bfloat16), preferred_element_type=jnp.float32
    ).astype(jnp.bfloat16)
    slot_hidden = jnp.einsum(
        "rck,sc->rsk", hidden, select_down.astype(jnp.bfloat16), preferred_element_type=jnp.float32
    ).astype(jnp.bfloat16)
    weight_terms = jnp.einsum(
        "rsk,rsj->skj", tokens_slots, slot_grad, preferred_element_type=jnp.float32
    )
    weight_terms = weight_terms + jnp.einsum(
        "rsk,rsj->skj", slot_hidden, cot_slots, preferred_element_type=jnp.float32
    )
    input_terms = block_inputs(slot_grad, block_weights, block_select)
    input_sum = lax.psum_scatter(input_terms, "cols", scatter_dimension=0, tiled=True)
    input_grad = input_sum.astype(jnp.bfloat16)
    weight_sum = lax.psum_scatter(
        weight_terms.astype(jnp.bfloat16), "dp", scatter_dimension=1, tiled=True
    )
    return (input_grad, weight_sum)


MESH = pl.DeviceIdType.MESH
F32 = jnp.float32
BF16 = jnp.bfloat16
NT = (((1,), (1,)), ((), ()))


def layer_kernel(
    n_cols, table_ref, slots_ref, tok_ref, cot_ref, w_ref, in_ref, wg_ref,
    tok, cot, blocks, wgu, wd, grads, hid, acc, sib_out, sib_in, chip_sum, a2a,
    fin_out, fin_in, lhs, hid_t,
    w_sem, own_sem, ring_send, ring_recv, sib_send, sib_recv,
    x_send, x_recv, half_send, half_recv, a2a_send, a2a_recv, fin_send, fin_recv,
):
    chips = n_cols // 2
    steps = chips // 2
    rows = tok_ref.shape[0]
    group_rows = rows * n_cols
    features = tok_ref.shape[1]
    width = blocks.shape[2]
    part = blocks.shape[1]
    n_f = features // width
    hidden = wd.shape[0]
    n_h = hidden // width
    zero_at = blocks.shape[0] - 1
    half = features // 2
    dp = lax.axis_index("dp")
    col = lax.axis_index("cols")
    core = col % 2
    chip = col // 2
    place = jnp.where(chip % 2 == 0, chip // 2, chips - 1 - chip // 2)

    def chip_at(p):
        p = (p + 2 * chips) % chips
        return jnp.where(p < steps, 2 * p, 2 * (chips - 1 - p) + 1)

    right = chip_at(place + 1) * 2 + core
    left = chip_at(place - 1) * 2 + core
    sibling = chip * 2 + 1 - core
    sides = ((tok_ref, tok), (cot_ref, cot))

    barrier = pltpu.get_barrier_semaphore()
    for r in range(1, chips):
        pl.semaphore_signal(barrier, inc=1, device_id=(dp, ((chip + r) % chips) * 2 + core), device_id_type=MESH)
    pl.semaphore_signal(barrier, inc=1, device_id=(dp, sibling), device_id_type=MESH)
    pl.semaphore_signal(barrier, inc=1, device_id=(1 - dp, col), device_id_type=MESH)
    pl.semaphore_wait(barrier, chips + 1)

    w_copy = pltpu.make_async_copy(w_ref, blocks.at[pl.ds(0, w_ref.shape[0])], w_sem)
    w_copy.start()

    def ring(g, direction, s, a):
        origin = chip_at(place - s if direction == 0 else place + s) * 2 + core
        block = sides[a][1].at[g, origin]
        return pltpu.make_async_remote_copy(
            src_ref=block, dst_ref=block,
            send_sem=ring_send.at[g, direction, s, a], recv_sem=ring_recv.at[g, direction, s, a],
            device_id=(dp, right if direction == 0 else left), device_id_type=MESH,
        )

    def ring_arrival(g, direction, s, a):
        origin = chip_at(place - 1 - s if direction == 0 else place + 1 + s) * 2 + core
        block = sides[a][1].at[g, origin]
        return pltpu.make_async_remote_copy(
            src_ref=block, dst_ref=block,
            send_sem=ring_send.at[g, direction, s, a], recv_sem=ring_recv.at[g, direction, s, a],
            device_id=(dp, right if direction == 0 else left), device_id_type=MESH,
        )

    def share(g, k, a, lane):
        origin = chip_at(place - k) * 2 + lane
        block = sides[a][1].at[g, origin]
        return pltpu.make_async_remote_copy(
            src_ref=block, dst_ref=block,
            send_sem=sib_send.at[g, k, a], recv_sem=sib_recv.at[g, k, a],
            device_id=(dp, sibling), device_id_type=MESH,
        )

    def cross(a):
        return pltpu.make_async_remote_copy(
            src_ref=sides[a][1].at[0, col], dst_ref=sides[a][1].at[1, col],
            send_sem=x_send.at[a], recv_sem=x_recv.at[a],
            device_id=(1 - dp, col), device_id_type=MESH,
        )

    def first(g):
        for a in range(2):
            for direction in range(2):
                ring(g, direction, 0, a).start()
        for a in range(2):
            share(g, 0, a, core).start()

    def pass_on(g, s, direction, a):
        ring_arrival(g, direction, s, a).wait_recv()

        far = steps - 1 if a == direction else steps - 2

        @pl.when(s < far)
        def _():
            ring(g, direction, s + 1, a).start()

        k = 1 + s if direction == 0 else chips - 1 - s
        share(g, k, a, core).start()

    def advance(g, s):
        pass_on(g, s, 0, 0)
        pass_on(g, s, 1, 1)

        @pl.when(s < steps - 1)
        def _():
            pass_on(g, s, 0, 1)
            pass_on(g, s, 1, 0)

    def all_shared(g):
        for a in range(2):
            @pl.loop(0, chips)
            def _(k):
                share(g, k, a, 1 - core).wait_recv()

    for a in range(2):
        own = pltpu.make_async_copy(sides[a][0], sides[a][1].at[0, col], own_sem.at[a])
        own.start()
        own.wait()
    first(0)
    cross(0).start()
    cross(1).start()
    blocks[zero_at] = jnp.zeros((part, width), BF16)
    w_copy.wait()

    pieces = width // part

    def spread(h, f):
        at = pl.multiple_of(f * width, width)
        hid_at = pl.multiple_of(h * width, width)
        for k in range(3):
            index = table_ref[(k * n_h + h) * n_f + f]
            for piece in range(pieces):
                value = blocks[jnp.minimum(index * pieces + piece, zero_at)]
                if k < 2:
                    wgu[pl.ds(pl.multiple_of(at + piece * part, part), part),
                        pl.ds(pl.multiple_of(k * hidden + hid_at, width), width)] = value
                else:
                    wd[pl.ds(pl.multiple_of(hid_at + piece * part, part), part), pl.ds(at, width)] = value

    per_step = n_h // steps

    @pl.loop(0, steps)
    def _(s):
        @pl.loop(0, n_f)
        def _(f):
            for j in range(per_step):
                spread(s * per_step + j, f)

        advance(0, s)

    all_shared(0)
    for a in range(2):
        cross(a).wait_recv()
    first(1)

    span = hidden // steps

    def forward(g, n):
        at = pl.multiple_of(n * span, span)
        x = tok[g].reshape(group_rows, features)
        gate = jnp.dot(x, wgu[:, pl.ds(at, span)], preferred_element_type=F32)
        up = jnp.dot(x, wgu[:, pl.ds(pl.multiple_of(hidden + at, span), span)], preferred_element_type=F32)
        back = lax.dot_general(
            cot[g].reshape(group_rows, features), wd[pl.ds(at, span), :], NT, preferred_element_type=F32
        )
        sig = jax.nn.sigmoid(gate)
        silu = gate * sig
        hid[g, :, pl.ds(at, span)] = (silu * up).astype(BF16)
        grads[g, :, pl.ds(at, span)] = (back * up * sig * (1.0 + gate * (1.0 - sig))).astype(BF16)
        grads[g, :, pl.ds(pl.multiple_of(hidden + at, span), span)] = (back * silu).astype(BF16)

    @pl.loop(0, steps)
    def _(s):
        forward(0, s)
        advance(1, s)

    chunk = half // 4

    def terms(at):
        return lax.dot_general(grads[0], wgu[pl.ds(at, chunk), :], NT, preferred_element_type=F32)

    @pl.loop(0, 4)
    def _(i):
        at = pl.multiple_of(i * chunk, chunk)
        src = pl.multiple_of((1 - core) * half + at, chunk)
        sib_out[:, pl.ds(at, chunk)] = terms(src).astype(BF16)

    to_sibling = pltpu.make_async_remote_copy(
        src_ref=sib_out, dst_ref=sib_in, send_sem=half_send, recv_sem=half_recv,
        device_id=(dp, sibling), device_id_type=MESH,
    )
    to_sibling.start()

    @pl.loop(0, 4)
    def _(i):
        at = pl.multiple_of(i * chunk, chunk)
        acc[:, pl.ds(at, chunk)] = terms(pl.multiple_of(core * half + at, chunk))

    to_sibling.wait_recv()
    chip_rows = group_rows // chips

    @pl.loop(0, chips)
    def _(c):
        at = pl.ds(pl.multiple_of(c * chip_rows, chip_rows), chip_rows)
        total = acc[at, :] + sib_in[at, :].astype(F32)
        acc[at, :] = total
        chip_sum[c] = total.astype(BF16)

    def spread_sum(r):
        other = (chip + r) % chips
        return pltpu.make_async_remote_copy(
            src_ref=chip_sum.at[other], dst_ref=a2a.at[r],
            send_sem=a2a_send.at[r], recv_sem=a2a_recv.at[r],
            device_id=(dp, other * 2 + core), device_id_type=MESH,
        )

    @pl.loop(1, chips)
    def _(r):
        spread_sum(r).start()

    all_shared(1)

    @pl.loop(0, steps)
    def _(s):
        forward(1, s)

    def take_part(block):
        out = block[:part]
        for i in range(1, width // part):
            out = jnp.where(dp == i, block[i * part:(i + 1) * part], out)
        return out

    for g in range(2):
        for h in range(n_h):
            hid_t[pl.ds(h * part, part), pl.ds(g * group_rows, group_rows)] = take_part(
                hid[g, :, pl.ds(h * width, width)].T
            )
    four = 4

    @pl.loop(0, n_f // four)
    def _(i):
        at = pl.multiple_of(i * four * width, four * width)
        for g in range(2):
            for b in range(four):
                piece = tok[g, :, :, pl.ds(pl.multiple_of(at + b * width, width), width)]
                lhs[pl.ds(b * part, part), pl.ds(g * group_rows, group_rows)] = take_part(
                    piece.reshape(group_rows, width).T
                )
        for n in range(2 * n_h // 4):
            cut = slice(n * 4 * width, (n + 1) * 4 * width)
            out = jnp.dot(
                lhs[...], grads[:, :, cut].reshape(2 * group_rows, 4 * width), preferred_element_type=F32
            ).astype(BF16)
            for h in range(4):
                for b in range(four):
                    blocks[(n * 4 + h) * n_f + i * four + b] = out[
                        b * part:(b + 1) * part, h * width:(h + 1) * width
                    ]
        c = cot[:, :, :, pl.ds(at, four * width)].reshape(2 * group_rows, four * width)
        out = jnp.dot(hid_t[...], c, preferred_element_type=F32).astype(BF16)
        for h in range(n_h):
            for b in range(four):
                blocks[(2 * n_h + h) * n_f + i * four + b] = out[
                    h * part:(h + 1) * part, b * width:(b + 1) * width
                ]

    @pl.loop(0, wg_ref.shape[0], unroll=8)
    def _(s):
        wg_ref[s] = blocks[slots_ref[s]]

    @pl.loop(1, chips)
    def _(r):
        spread_sum(r).wait_recv()

    total = acc[pl.ds(pl.multiple_of(chip * chip_rows, chip_rows), chip_rows), :]
    for r in range(1, chips):
        total = total + a2a[r].astype(F32)
    total = total.astype(BF16)
    low, high = total[:rows], total[rows:]
    fin_out[...] = jnp.where(core == 0, high, low)
    fin = pltpu.make_async_remote_copy(
        src_ref=fin_out, dst_ref=fin_in, send_sem=fin_send, recv_sem=fin_recv,
        device_id=(dp, sibling), device_id_type=MESH,
    )
    fin.start()
    in_ref[:, pl.ds(pl.multiple_of(core * half, half), half)] = jnp.where(core == 0, low, high)
    fin.wait()
    in_ref[:, pl.ds(pl.multiple_of((1 - core) * half, half), half)] = fin_in[...]

    to_sibling.wait_send()

    @pl.loop(1, chips)
    def _(r):
        spread_sum(r).wait_send()

    for a in range(2):
        cross(a).wait_send()
    for g in range(2):
        for a in range(2):
            for direction in range(2):
                @pl.loop(0, steps if a == direction else steps - 1)
                def _(s):
                    ring(g, direction, s, a).wait_send()

            @pl.loop(0, chips)
            def _(k):
                share(g, k, a, core).wait_send()


def kernel_shards(n_cols, tokens, cotangent, block_weights, slot_block, slot_target, counts):
    n_slots, width = block_weights.shape[:2]
    n_dp = 2
    part = width // n_dp
    rows, features = tokens.shape
    n_f = features // width
    hidden_blocks = n_slots // SPC
    hidden = hidden_blocks * width
    places = 3 * hidden_blocks * n_f
    place = slot_target * n_f + slot_block
    number = jnp.arange(n_slots, dtype=jnp.int32)
    live = number < counts[0]
    hit = (place[None, :] == jnp.arange(places, dtype=jnp.int32)[:, None]) & live[None, :]
    table = places + jnp.sum(jnp.where(hit, number[None, :] - places, 0), axis=1)
    slots = jnp.where(live, place, places)
    chips = n_cols // 2
    group_rows = rows * n_cols
    half = features // 2
    dma = pltpu.SemaphoreType.DMA
    vmem = pl.BlockSpec(memory_space=pltpu.VMEM)
    smem = pl.BlockSpec(memory_space=pltpu.SMEM)
    return pl.pallas_call(
        functools.partial(layer_kernel, n_cols),
        out_shape=(
            jax.ShapeDtypeStruct((rows, features), BF16),
            jax.ShapeDtypeStruct((n_slots, part, width), BF16),
        ),
        in_specs=[smem, smem, vmem, vmem, pl.BlockSpec(memory_space=pl.ANY)],
        out_specs=(vmem, vmem),
        scratch_shapes=[
            pltpu.VMEM((n_dp, n_cols, rows, features), BF16),
            pltpu.VMEM((n_dp, n_cols, rows, features), BF16),
            pltpu.VMEM((places + 1, part, width), BF16),
            pltpu.VMEM((features, 2 * hidden), BF16),
            pltpu.VMEM((hidden, features), BF16),
            pltpu.VMEM((n_dp, group_rows, 2 * hidden), BF16),
            pltpu.VMEM((n_dp, group_rows, hidden), BF16),
            pltpu.VMEM((group_rows, half), F32),
            pltpu.VMEM((group_rows, half), BF16),
            pltpu.VMEM((group_rows, half), BF16),
            pltpu.VMEM((chips, group_rows // chips, half), BF16),
            pltpu.VMEM((chips, group_rows // chips, half), BF16),
            pltpu.VMEM((rows, half), BF16),
            pltpu.VMEM((rows, half), BF16),
            pltpu.VMEM((4 * part, n_dp * group_rows), BF16),
            pltpu.VMEM((hidden // n_dp, n_dp * group_rows), BF16),
            dma, dma((2,)),
            dma((2, 2, chips // 2, 2)), dma((2, 2, chips // 2, 2)),
            dma((2, chips, 2)), dma((2, chips, 2)),
            dma((2,)), dma((2,)), dma, dma, dma((chips,)), dma((chips,)), dma, dma,
        ],
        compiler_params=pltpu.CompilerParams(
            collective_id=0, has_side_effects=True, vmem_limit_bytes=67043328
        ),
    )(table, slots, tokens, cotangent, block_weights.reshape(n_slots * n_dp, part, width))


def solution(mesh):
    n_dp, n_cols = mesh.shape["dp"], mesh.shape["cols"]
    paired = n_dp == 2 and n_cols % 4 == 0

    def body(*args):
        tokens, weights = args[0], args[2]
        if paired and tokens.shape[0] % 16 == 0 and weights.shape[0] // SPC % (n_cols // 4) == 0:
            return kernel_shards(n_cols, *args)
        return shards(*args)

    return jax.shard_map(
        body,
        mesh=mesh,
        in_specs=(
            P(("dp", "cols"), None),
            P(("dp", "cols"), None),
            P("cols", None, None),
            P("cols"),
            P("cols"),
            P("cols"),
        ),
        out_specs=(P(("dp", "cols"), None), P("cols", "dp", None)),
        check_vma=False,
    )
```

```python
import functools

import jax
import jax.numpy as jnp
from jax import lax
from jax.experimental import pallas as pl
from jax.experimental.pallas import tpu as pltpu
from jax.sharding import PartitionSpec as P

SPC = 32


def block_inputs(grad_rows, weights, block_select):
    partial_rows = jnp.einsum(
        "rsj,skj->rsk", grad_rows, weights, preferred_element_type=jnp.float32
    )
    summed = jnp.einsum("rsk,sb->rbk", partial_rows, block_select)
    return summed.reshape(summed.shape[0], summed.shape[1] * summed.shape[2])


def shards(tokens, cotangent, block_weights, slot_block, slot_target, counts):
    slot_total = block_weights.shape[0]
    block_width = block_weights.shape[1]
    columns = slot_total // SPC
    features = tokens.shape[1]
    block_count = features // block_width
    tokens_all, cot_all = (
        lax.all_gather(tokens, "cols", axis=0, tiled=True),
        lax.all_gather(cotangent, "cols", axis=0, tiled=True),
    )
    row_total = tokens_all.shape[0]
    live_slot = jnp.arange(slot_total) < counts[0]
    slot_kind = slot_target // columns
    places = slot_target % columns
    up_mask = (live_slot & (slot_kind < 2))[:, None].astype(jnp.float32)
    down_mask = (live_slot & (slot_kind == 2))[:, None].astype(jnp.float32)
    select_up = jax.nn.one_hot(slot_target, 2 * columns, dtype=jnp.float32) * up_mask
    select_down = jax.nn.one_hot(places, columns, dtype=jnp.float32) * down_mask
    block_select = jax.nn.one_hot(slot_block, block_count, dtype=jnp.float32)
    tokens_slots = jnp.take(
        tokens_all.reshape(row_total, block_count, block_width), slot_block, axis=1
    )
    products = jnp.einsum(
        "rsk,skj->rsj", tokens_slots, block_weights, preferred_element_type=jnp.float32
    )
    gate_up = jnp.einsum("rsj,sc->rcj", products, select_up)
    gate_pre = gate_up[:, :columns]
    up_pre = gate_up[:, columns:]
    sigmoid_gate = jax.nn.sigmoid(gate_pre)
    silu_gate = gate_pre * sigmoid_gate
    hidden = (silu_gate * up_pre).astype(jnp.bfloat16)
    cot_slots = jnp.take(cot_all.reshape(row_total, block_count, block_width), slot_block, axis=1)
    back_products = jnp.einsum(
        "rsj,skj->rsk", cot_slots, block_weights, preferred_element_type=jnp.float32
    )
    hidden_grad = jnp.einsum("rsk,sc->rck", back_products, select_down)
    gate_grad = (
        hidden_grad * up_pre * sigmoid_gate * (1.0 + gate_pre * (1.0 - sigmoid_gate))
    ).astype(jnp.bfloat16)
    up_grad = (hidden_grad * silu_gate).astype(jnp.bfloat16)
    pre_grad = jnp.concatenate([gate_grad, up_grad], axis=1)
    slot_grad = jnp.einsum(
        "rck,sc->rsk", pre_grad, select_up.astype(jnp.bfloat16), preferred_element_type=jnp.float32
    ).astype(jnp.bfloat16)
    slot_hidden = jnp.einsum(
        "rck,sc->rsk", hidden, select_down.astype(jnp.bfloat16), preferred_element_type=jnp.float32
    ).astype(jnp.bfloat16)
    weight_terms = jnp.einsum(
        "rsk,rsj->skj", tokens_slots, slot_grad, preferred_element_type=jnp.float32
    )
    weight_terms = weight_terms + jnp.einsum(
        "rsk,rsj->skj", slot_hidden, cot_slots, preferred_element_type=jnp.float32
    )
    input_terms = block_inputs(slot_grad, block_weights, block_select)
    input_sum = lax.psum_scatter(input_terms, "cols", scatter_dimension=0, tiled=True)
    input_grad = input_sum.astype(jnp.bfloat16)
    weight_sum = lax.psum_scatter(
        weight_terms.astype(jnp.bfloat16), "dp", scatter_dimension=1, tiled=True
    )
    return (input_grad, weight_sum)


MESH = pl.DeviceIdType.MESH
F32 = jnp.float32
BF16 = jnp.bfloat16
NT = (((1,), (1,)), ((), ()))
CHUNKS = 4


def layer_kernel(
    n_cols, table_ref, slots_ref, tok_ref, cot_ref, w_ref, in_ref, wg_ref,
    tok, cot, blocks, wgu, wd, grads, hid, pre, acc, sib_out, sib_in, chip_sum, a2a,
    fin_out, fin_in, lhs, hid_t,
    w_sem, own_sem, ring_send, ring_recv, sib_send, sib_recv,
    x_send, x_recv, half_send, half_recv, a2a_send, a2a_recv, fin_send, fin_recv,
):
    chips = n_cols // 2
    steps = chips // 2
    rows = tok_ref.shape[0]
    group_rows = rows * n_cols
    features = tok_ref.shape[1]
    width = blocks.shape[2]
    part = blocks.shape[1]
    n_f = features // width
    hidden = wd.shape[0]
    n_h = hidden // width
    zero_at = blocks.shape[0] - 1
    half = features // 2
    dp = lax.axis_index("dp")
    col = lax.axis_index("cols")
    core = col % 2
    chip = col // 2
    place = jnp.where(chip % 2 == 0, chip // 2, chips - 1 - chip // 2)

    def chip_at(p):
        p = (p + 2 * chips) % chips
        return jnp.where(p < steps, 2 * p, 2 * (chips - 1 - p) + 1)

    right = chip_at(place + 1) * 2 + core
    left = chip_at(place - 1) * 2 + core
    sibling = chip * 2 + 1 - core
    sides = ((tok_ref, tok), (cot_ref, cot))

    barrier = pltpu.get_barrier_semaphore()
    for r in range(1, chips):
        pl.semaphore_signal(barrier, inc=1, device_id=(dp, ((chip + r) % chips) * 2 + core), device_id_type=MESH)
    pl.semaphore_signal(barrier, inc=1, device_id=(dp, sibling), device_id_type=MESH)
    pl.semaphore_signal(barrier, inc=1, device_id=(1 - dp, col), device_id_type=MESH)
    pl.semaphore_wait(barrier, chips + 1)

    w_copy = pltpu.make_async_copy(w_ref, blocks.at[pl.ds(0, w_ref.shape[0])], w_sem)
    w_copy.start()

    def piece(g, origin, a):
        at = pl.ds((a % 2) * half, half)
        return sides[a // 2][1].at[g, origin * 2 + core, :, at]

    def ring_copy(g, origin, direction, s, a):
        block = piece(g, origin, a)
        return pltpu.make_async_remote_copy(
            src_ref=block, dst_ref=block,
            send_sem=ring_send.at[g, direction, s, a], recv_sem=ring_recv.at[g, direction, s, a],
            device_id=(dp, right if direction == 0 else left), device_id_type=MESH,
        )

    def ring(g, direction, s, a):
        return ring_copy(g, chip_at(place - s if direction == 0 else place + s), direction, s, a)

    def ring_arrival(g, direction, s, a):
        return ring_copy(g, chip_at(place - 1 - s if direction == 0 else place + 1 + s), direction, s, a)

    def share_copy(g, k, a, lane):
        at = pl.ds((a % 2) * half, half)
        block = sides[a // 2][1].at[g, chip_at(place - k) * 2 + lane, :, at]
        return pltpu.make_async_remote_copy(
            src_ref=block, dst_ref=block,
            send_sem=sib_send.at[g, k, a], recv_sem=sib_recv.at[g, k, a],
            device_id=(dp, sibling), device_id_type=MESH,
        )

    def share(g, k, a):
        return share_copy(g, k, a, core)

    def cross(k, a):
        origin = chip_at(place - k)
        return pltpu.make_async_remote_copy(
            src_ref=piece(0, origin, a), dst_ref=piece(1, origin, a),
            send_sem=x_send.at[k, a], recv_sem=x_recv.at[k, a],
            device_id=(1 - dp, col), device_id_type=MESH,
        )

    def first(g, arr):
        for a in (2 * arr, 2 * arr + 1):
            for direction in range(2):
                ring(g, direction, 0, a).start()
        for a in (2 * arr, 2 * arr + 1):
            share(g, 0, a).start()
            if g == 0:
                cross(0, a).start()

    def pass_on(s, direction, a):
        ring_arrival(0, direction, s, a).wait_recv()

        far = steps - 1 if a % 2 == direction else steps - 2

        @pl.when(s < far)
        def _():
            ring(0, direction, s + 1, a).start()

        k = 1 + s if direction == 0 else chips - 1 - s
        share(0, k, a).start()

        @pl.when(s > 0)
        def _():
            cross(k, a).start()

    def advance(s, arr):
        for direction in range(2):
            pass_on(s, direction, 2 * arr + direction)

        @pl.when(s < steps - 1)
        def _():
            for direction in range(2):
                pass_on(s, direction, 2 * arr + 1 - direction)

    def all_shared(g, arr):
        @pl.loop(0, chips)
        def _(k):
            for a in (2 * arr, 2 * arr + 1):
                share_copy(g, k, a, 1 - core).wait_recv()

    def crossed(k):
        for a in range(4):
            cross(k, a).wait_recv()
            share(1, k, a).start()

    for a in range(2):
        own = pltpu.make_async_copy(sides[a][0], sides[a][1].at[0, col], own_sem.at[a])
        own.start()
        own.wait()
    first(0, 0)
    blocks[zero_at] = jnp.zeros((part, width), BF16)
    w_copy.wait()

    pieces = width // part

    def spread(h, f):
        at = pl.multiple_of(f * width, width)
        hid_at = pl.multiple_of(h * width, width)
        for k in range(3):
            index = table_ref[(k * n_h + h) * n_f + f]
            for piece in range(pieces):
                value = blocks[jnp.minimum(index * pieces + piece, zero_at)]
                if k < 2:
                    wgu[pl.ds(pl.multiple_of(at + piece * part, part), part),
                        pl.ds(pl.multiple_of(k * hidden + hid_at, width), width)] = value
                else:
                    wd[pl.ds(pl.multiple_of(hid_at + piece * part, part), part), pl.ds(at, width)] = value

    per_step = n_h // steps

    @pl.loop(0, steps)
    def _(s):
        @pl.loop(0, n_f)
        def _(f):
            for j in range(per_step):
                spread(s * per_step + j, f)

        advance(s, 0)

        @pl.when(s == steps // 2 - 1)
        def _():
            first(0, 1)

    all_shared(0, 0)
    span = hidden // steps

    def before(g, n):
        at = pl.multiple_of(n * span, span)
        x = tok[g].reshape(group_rows, features)
        gate = jnp.dot(x, wgu[:, pl.ds(at, span)], preferred_element_type=F32)
        up = jnp.dot(x, wgu[:, pl.ds(pl.multiple_of(hidden + at, span), span)], preferred_element_type=F32)
        return gate, up

    def after(g, n, gate, up):
        at = pl.multiple_of(n * span, span)
        back = lax.dot_general(
            cot[g].reshape(group_rows, features), wd[pl.ds(at, span), :], NT, preferred_element_type=F32
        )
        sig = jax.nn.sigmoid(gate)
        silu = gate * sig
        hid[g, :, pl.ds(at, span)] = (silu * up).astype(BF16)
        grads[g, :, pl.ds(at, span)] = (back * up * sig * (1.0 + gate * (1.0 - sig))).astype(BF16)
        grads[g, :, pl.ds(pl.multiple_of(hidden + at, span), span)] = (back * silu).astype(BF16)

    @pl.loop(0, steps)
    def _(s):
        gate, up = before(0, s)
        pre[s, 0] = gate
        pre[s, 1] = up
        advance(s, 1)

    for a in range(4):
        cross(0, a).wait_recv()
    first(1, 0)
    first(1, 1)
    all_shared(0, 1)

    @pl.loop(0, steps)
    def _(s):
        after(0, s, pre[s, 0], pre[s, 1])

    crossed(2)
    crossed(chips - 2)

    chunk = half // CHUNKS
    chip_rows = group_rows // chips

    def terms(at):
        return lax.dot_general(grads[0], wgu[pl.ds(at, chunk), :], NT, preferred_element_type=F32)

    def to_sibling(i):
        return pltpu.make_async_remote_copy(
            src_ref=sib_out.at[i], dst_ref=sib_in.at[i], send_sem=half_send.at[i], recv_sem=half_recv.at[i],
            device_id=(dp, sibling), device_id_type=MESH,
        )

    def spread_sum(r, i):
        other = (chip + r) % chips
        return pltpu.make_async_remote_copy(
            src_ref=chip_sum.at[i, other], dst_ref=a2a.at[i, r],
            send_sem=a2a_send.at[i, r], recv_sem=a2a_recv.at[i, r],
            device_id=(dp, other * 2 + core), device_id_type=MESH,
        )

    def pair_sum(i):
        to_sibling(i).wait_recv()

        @pl.loop(0, chips)
        def _(c):
            at = pl.ds(pl.multiple_of(c * chip_rows, chip_rows), chip_rows)
            total = acc[i, at, :] + sib_in[i, at, :].astype(F32)
            acc[i, at, :] = total
            chip_sum[i, c] = total.astype(BF16)

        @pl.loop(1, chips)
        def _(r):
            spread_sum(r, i).start()

    @pl.loop(0, CHUNKS)
    def _(i):
        at = pl.multiple_of(i * chunk, chunk)
        sib_out[i] = terms(pl.multiple_of((1 - core) * half + at, chunk)).astype(BF16)
        to_sibling(i).start()
        acc[i] = terms(pl.multiple_of(core * half + at, chunk))

        @pl.when(i > 0)
        def _():
            pair_sum(i - 1)

    pair_sum(CHUNKS - 1)

    for direction in range(2):
        for a in range(4):
            ring_arrival(1, direction, 0, a).wait_recv()
            share(1, 1 if direction == 0 else chips - 1, a).start()

    @pl.loop(3, chips - 2)
    def _(k):
        crossed(k)

    all_shared(1, 0)
    all_shared(1, 1)

    @pl.loop(0, steps)
    def _(s):
        gate, up = before(1, s)
        after(1, s, gate, up)

    def take_part(block):
        out = block[:part]
        for i in range(1, width // part):
            out = jnp.where(dp == i, block[i * part:(i + 1) * part], out)
        return out

    for g in range(2):
        for h in range(n_h):
            hid_t[pl.ds(h * part, part), pl.ds(g * group_rows, group_rows)] = take_part(
                hid[g, :, pl.ds(h * width, width)].T
            )
    four = 4

    @pl.loop(0, n_f // four)
    def _(i):
        at = pl.multiple_of(i * four * width, four * width)
        for g in range(2):
            for b in range(four):
                piece = tok[g, :, :, pl.ds(pl.multiple_of(at + b * width, width), width)]
                lhs[pl.ds(b * part, part), pl.ds(g * group_rows, group_rows)] = take_part(
                    piece.reshape(group_rows, width).T
                )
        for n in range(2 * n_h // 4):
            cut = slice(n * 4 * width, (n + 1) * 4 * width)
            out = jnp.dot(
                lhs[...], grads[:, :, cut].reshape(2 * group_rows, 4 * width), preferred_element_type=F32
            ).astype(BF16)
            for h in range(4):
                for b in range(four):
                    blocks[(n * 4 + h) * n_f + i * four + b] = out[
                        b * part:(b + 1) * part, h * width:(h + 1) * width
                    ]
        c = cot[:, :, :, pl.ds(at, four * width)].reshape(2 * group_rows, four * width)
        out = jnp.dot(hid_t[...], c, preferred_element_type=F32).astype(BF16)
        for h in range(n_h):
            for b in range(four):
                blocks[(2 * n_h + h) * n_f + i * four + b] = out[
                    h * part:(h + 1) * part, b * width:(b + 1) * width
                ]

    @pl.loop(0, wg_ref.shape[0], unroll=8)
    def _(s):
        wg_ref[s] = blocks[slots_ref[s]]

    mine = pl.ds(pl.multiple_of(chip * chip_rows, chip_rows), chip_rows)

    @pl.loop(0, CHUNKS)
    def _(i):
        total = acc[i, mine, :]
        for r in range(1, chips):
            spread_sum(r, i).wait_recv()
            total = total + a2a[i, r].astype(F32)
        total = total.astype(BF16)
        low, high = total[:rows], total[rows:]
        at = pl.multiple_of(i * chunk, chunk)
        fin_out[:, pl.ds(at, chunk)] = jnp.where(core == 0, high, low)
        in_ref[:, pl.ds(pl.multiple_of(core * half + at, chunk), chunk)] = jnp.where(core == 0, low, high)

    fin = pltpu.make_async_remote_copy(
        src_ref=fin_out, dst_ref=fin_in, send_sem=fin_send, recv_sem=fin_recv,
        device_id=(dp, sibling), device_id_type=MESH,
    )
    fin.start()

    @pl.loop(0, CHUNKS)
    def _(i):
        to_sibling(i).wait_send()

        @pl.loop(1, chips)
        def _(r):
            spread_sum(r, i).wait_send()

    for a in range(4):
        @pl.loop(0, chips)
        def _(k):
            share(0, k, a).wait_send()
            share(1, k, a).wait_send()

        cross(0, a).wait_send()

        @pl.loop(2, chips - 1)
        def _(k):
            cross(k, a).wait_send()

        for direction in range(2):
            @pl.loop(0, steps if a % 2 == direction else steps - 1)
            def _(s):
                ring(0, direction, s, a).wait_send()

            ring(1, direction, 0, a).wait_send()

    fin.wait()
    in_ref[:, pl.ds(pl.multiple_of((1 - core) * half, half), half)] = fin_in[...]


def kernel_shards(n_cols, tokens, cotangent, block_weights, slot_block, slot_target, counts):
    n_slots, width = block_weights.shape[:2]
    n_dp = 2
    part = width // n_dp
    rows, features = tokens.shape
    n_f = features // width
    hidden_blocks = n_slots // SPC
    hidden = hidden_blocks * width
    places = 3 * hidden_blocks * n_f
    place = slot_target * n_f + slot_block
    number = jnp.arange(n_slots, dtype=jnp.int32)
    live = number < counts[0]
    hit = (place[None, :] == jnp.arange(places, dtype=jnp.int32)[:, None]) & live[None, :]
    table = places + jnp.sum(jnp.where(hit, number[None, :] - places, 0), axis=1)
    slots = jnp.where(live, place, places)
    chips = n_cols // 2
    group_rows = rows * n_cols
    half = features // 2
    dma = pltpu.SemaphoreType.DMA
    vmem = pl.BlockSpec(memory_space=pltpu.VMEM)
    smem = pl.BlockSpec(memory_space=pltpu.SMEM)
    return pl.pallas_call(
        functools.partial(layer_kernel, n_cols),
        out_shape=(
            jax.ShapeDtypeStruct((rows, features), BF16),
            jax.ShapeDtypeStruct((n_slots, part, width), BF16),
        ),
        in_specs=[smem, smem, vmem, vmem, pl.BlockSpec(memory_space=pl.ANY)],
        out_specs=(vmem, vmem),
        scratch_shapes=[
            pltpu.VMEM((n_dp, n_cols, rows, features), BF16),
            pltpu.VMEM((n_dp, n_cols, rows, features), BF16),
            pltpu.VMEM((places + 1, part, width), BF16),
            pltpu.VMEM((features, 2 * hidden), BF16),
            pltpu.VMEM((hidden, features), BF16),
            pltpu.VMEM((n_dp, group_rows, 2 * hidden), BF16),
            pltpu.VMEM((n_dp, group_rows, hidden), BF16),
            pltpu.VMEM((chips // 2, 2, group_rows, hidden // (chips // 2)), F32),
            pltpu.VMEM((CHUNKS, group_rows, half // CHUNKS), F32),
            pltpu.VMEM((CHUNKS, group_rows, half // CHUNKS), BF16),
            pltpu.VMEM((CHUNKS, group_rows, half // CHUNKS), BF16),
            pltpu.VMEM((CHUNKS, chips, group_rows // chips, half // CHUNKS), BF16),
            pltpu.VMEM((CHUNKS, chips, group_rows // chips, half // CHUNKS), BF16),
            pltpu.VMEM((rows, half), BF16),
            pltpu.VMEM((rows, half), BF16),
            pltpu.VMEM((4 * part, n_dp * group_rows), BF16),
            pltpu.VMEM((hidden // n_dp, n_dp * group_rows), BF16),
            dma, dma((2,)),
            dma((2, 2, chips // 2, 4)), dma((2, 2, chips // 2, 4)),
            dma((2, chips, 4)), dma((2, chips, 4)),
            dma((chips, 4)), dma((chips, 4)), dma((CHUNKS,)), dma((CHUNKS,)),
            dma((CHUNKS, chips)), dma((CHUNKS, chips)), dma, dma,
        ],
        compiler_params=pltpu.CompilerParams(
            collective_id=0, has_side_effects=True, vmem_limit_bytes=67043328
        ),
    )(table, slots, tokens, cotangent, block_weights.reshape(n_slots * n_dp, part, width))


def solution(mesh):
    n_dp, n_cols = mesh.shape["dp"], mesh.shape["cols"]
    paired = n_dp == 2 and n_cols % 4 == 0

    def body(*args):
        tokens, weights = args[0], args[2]
        if paired and tokens.shape[0] % 16 == 0 and weights.shape[0] // SPC % (n_cols // 4) == 0:
            return kernel_shards(n_cols, *args)
        return shards(*args)

    return jax.shard_map(
        body,
        mesh=mesh,
        in_specs=(
            P(("dp", "cols"), None),
            P(("dp", "cols"), None),
            P("cols", None, None),
            P("cols"),
            P("cols"),
            P("cols"),
        ),
        out_specs=(P(("dp", "cols"), None), P("cols", "dp", None)),
        check_vma=False,
    )
```

```python
import functools

import jax
import jax.numpy as jnp
from jax import lax
from jax.experimental import pallas as pl
from jax.experimental.pallas import tpu as pltpu
from jax.sharding import PartitionSpec as P

SPC = 32


def block_inputs(grad_rows, weights, block_select):
    partial_rows = jnp.einsum(
        "rsj,skj->rsk", grad_rows, weights, preferred_element_type=jnp.float32
    )
    summed = jnp.einsum("rsk,sb->rbk", partial_rows, block_select)
    return summed.reshape(summed.shape[0], summed.shape[1] * summed.shape[2])


def shards(tokens, cotangent, block_weights, slot_block, slot_target, counts):
    slot_total = block_weights.shape[0]
    block_width = block_weights.shape[1]
    columns = slot_total // SPC
    features = tokens.shape[1]
    block_count = features // block_width
    tokens_all, cot_all = (
        lax.all_gather(tokens, "cols", axis=0, tiled=True),
        lax.all_gather(cotangent, "cols", axis=0, tiled=True),
    )
    row_total = tokens_all.shape[0]
    live_slot = jnp.arange(slot_total) < counts[0]
    slot_kind = slot_target // columns
    places = slot_target % columns
    up_mask = (live_slot & (slot_kind < 2))[:, None].astype(jnp.float32)
    down_mask = (live_slot & (slot_kind == 2))[:, None].astype(jnp.float32)
    select_up = jax.nn.one_hot(slot_target, 2 * columns, dtype=jnp.float32) * up_mask
    select_down = jax.nn.one_hot(places, columns, dtype=jnp.float32) * down_mask
    block_select = jax.nn.one_hot(slot_block, block_count, dtype=jnp.float32)
    tokens_slots = jnp.take(
        tokens_all.reshape(row_total, block_count, block_width), slot_block, axis=1
    )
    products = jnp.einsum(
        "rsk,skj->rsj", tokens_slots, block_weights, preferred_element_type=jnp.float32
    )
    gate_up = jnp.einsum("rsj,sc->rcj", products, select_up)
    gate_pre = gate_up[:, :columns]
    up_pre = gate_up[:, columns:]
    sigmoid_gate = jax.nn.sigmoid(gate_pre)
    silu_gate = gate_pre * sigmoid_gate
    hidden = (silu_gate * up_pre).astype(jnp.bfloat16)
    cot_slots = jnp.take(cot_all.reshape(row_total, block_count, block_width), slot_block, axis=1)
    back_products = jnp.einsum(
        "rsj,skj->rsk", cot_slots, block_weights, preferred_element_type=jnp.float32
    )
    hidden_grad = jnp.einsum("rsk,sc->rck", back_products, select_down)
    gate_grad = (
        hidden_grad * up_pre * sigmoid_gate * (1.0 + gate_pre * (1.0 - sigmoid_gate))
    ).astype(jnp.bfloat16)
    up_grad = (hidden_grad * silu_gate).astype(jnp.bfloat16)
    pre_grad = jnp.concatenate([gate_grad, up_grad], axis=1)
    slot_grad = jnp.einsum(
        "rck,sc->rsk", pre_grad, select_up.astype(jnp.bfloat16), preferred_element_type=jnp.float32
    ).astype(jnp.bfloat16)
    slot_hidden = jnp.einsum(
        "rck,sc->rsk", hidden, select_down.astype(jnp.bfloat16), preferred_element_type=jnp.float32
    ).astype(jnp.bfloat16)
    weight_terms = jnp.einsum(
        "rsk,rsj->skj", tokens_slots, slot_grad, preferred_element_type=jnp.float32
    )
    weight_terms = weight_terms + jnp.einsum(
        "rsk,rsj->skj", slot_hidden, cot_slots, preferred_element_type=jnp.float32
    )
    input_terms = block_inputs(slot_grad, block_weights, block_select)
    input_sum = lax.psum_scatter(input_terms, "cols", scatter_dimension=0, tiled=True)
    input_grad = input_sum.astype(jnp.bfloat16)
    weight_sum = lax.psum_scatter(
        weight_terms.astype(jnp.bfloat16), "dp", scatter_dimension=1, tiled=True
    )
    return (input_grad, weight_sum)


MESH = pl.DeviceIdType.MESH
F32 = jnp.float32
BF16 = jnp.bfloat16
NT = (((1,), (1,)), ((), ()))
CHUNKS = 4


def layer_kernel(
    n_cols, table_ref, slots_ref, tok_ref, cot_ref, w_ref, in_ref, wg_ref,
    tok, cot, blocks, wgu, wd, grads, hid, pre, acc, sib_out, sib_in, chip_sum, a2a,
    fin_out, fin_in, lhs, hid_t,
    w_sem, own_sem, ring_send, ring_recv, sib_send, sib_recv,
    x_send, x_recv, half_send, half_recv, a2a_send, a2a_recv, fin_send, fin_recv,
):
    chips = n_cols // 2
    steps = chips // 2
    rows = tok_ref.shape[0]
    group_rows = rows * n_cols
    features = tok_ref.shape[1]
    width = blocks.shape[2]
    part = blocks.shape[1]
    n_f = features // width
    hidden = wd.shape[0]
    n_h = hidden // width
    zero_at = blocks.shape[0] - 1
    half = features // 2
    dp = lax.axis_index("dp")
    col = lax.axis_index("cols")
    core = col % 2
    chip = col // 2
    place = jnp.where(chip % 2 == 0, chip // 2, chips - 1 - chip // 2)

    def chip_at(p):
        p = (p + 2 * chips) % chips
        return jnp.where(p < steps, 2 * p, 2 * (chips - 1 - p) + 1)

    right = chip_at(place + 1) * 2 + core
    left = chip_at(place - 1) * 2 + core
    sibling = chip * 2 + 1 - core
    sides = ((tok_ref, tok), (cot_ref, cot))

    owns = [pltpu.make_async_copy(sides[a][0], sides[a][1].at[0, col], own_sem.at[a]) for a in range(2)]
    for own in owns:
        own.start()
    w_copy = pltpu.make_async_copy(w_ref, blocks.at[pl.ds(0, w_ref.shape[0])], w_sem)
    w_copy.start()
    barrier = pltpu.get_barrier_semaphore()
    for r in range(1, chips):
        pl.semaphore_signal(barrier, inc=1, device_id=(dp, ((chip + r) % chips) * 2 + core), device_id_type=MESH)
    pl.semaphore_signal(barrier, inc=1, device_id=(dp, sibling), device_id_type=MESH)
    pl.semaphore_signal(barrier, inc=1, device_id=(1 - dp, col), device_id_type=MESH)
    pl.semaphore_wait(barrier, chips + 1)

    def piece(g, origin, a):
        at = pl.ds((a % 2) * half, half)
        return sides[a // 2][1].at[g, origin * 2 + core, :, at]

    def ring_copy(g, origin, direction, s, a):
        block = piece(g, origin, a)
        return pltpu.make_async_remote_copy(
            src_ref=block, dst_ref=block,
            send_sem=ring_send.at[g, direction, s, a], recv_sem=ring_recv.at[g, direction, s, a],
            device_id=(dp, right if direction == 0 else left), device_id_type=MESH,
        )

    def ring(g, direction, s, a):
        return ring_copy(g, chip_at(place - s if direction == 0 else place + s), direction, s, a)

    def ring_arrival(g, direction, s, a):
        return ring_copy(g, chip_at(place - 1 - s if direction == 0 else place + 1 + s), direction, s, a)

    def share_copy(g, k, a, lane):
        at = pl.ds((a % 2) * half, half)
        block = sides[a // 2][1].at[g, chip_at(place - k) * 2 + lane, :, at]
        return pltpu.make_async_remote_copy(
            src_ref=block, dst_ref=block,
            send_sem=sib_send.at[g, k, a], recv_sem=sib_recv.at[g, k, a],
            device_id=(dp, sibling), device_id_type=MESH,
        )

    def share(g, k, a):
        return share_copy(g, k, a, core)

    def cross(k, a):
        origin = chip_at(place - k)
        return pltpu.make_async_remote_copy(
            src_ref=piece(0, origin, a), dst_ref=piece(1, origin, a),
            send_sem=x_send.at[k, a], recv_sem=x_recv.at[k, a],
            device_id=(1 - dp, col), device_id_type=MESH,
        )

    def first(g, arr):
        for a in (2 * arr, 2 * arr + 1):
            for direction in range(2):
                ring(g, direction, 0, a).start()
        for a in (2 * arr, 2 * arr + 1):
            share(g, 0, a).start()
            if g == 0:
                cross(0, a).start()

    def pass_on(s, direction, a):
        ring_arrival(0, direction, s, a).wait_recv()

        far = steps - 1 if a % 2 == direction else steps - 2

        @pl.when(s < far)
        def _():
            ring(0, direction, s + 1, a).start()

        k = 1 + s if direction == 0 else chips - 1 - s
        share(0, k, a).start()

        @pl.when(s > 0)
        def _():
            cross(k, a).start()

    def advance(s, arr):
        for direction in range(2):
            pass_on(s, direction, 2 * arr + direction)

        @pl.when(s < steps - 1)
        def _():
            for direction in range(2):
                pass_on(s, direction, 2 * arr + 1 - direction)

    def all_shared(g, arr):
        @pl.loop(0, chips)
        def _(k):
            for a in (2 * arr, 2 * arr + 1):
                share_copy(g, k, a, 1 - core).wait_recv()

    def crossed(k):
        for a in range(4):
            cross(k, a).wait_recv()
            share(1, k, a).start()

    for own in owns:
        own.wait()
    first(0, 0)
    blocks[zero_at] = jnp.zeros((part, width), BF16)
    w_copy.wait()

    pieces = width // part

    def spread(h, f):
        at = pl.multiple_of(f * width, width)
        hid_at = pl.multiple_of(h * width, width)
        for k in range(3):
            index = table_ref[(k * n_h + h) * n_f + f]
            for piece in range(pieces):
                value = blocks[jnp.minimum(index * pieces + piece, zero_at)]
                if k < 2:
                    wgu[pl.ds(pl.multiple_of(at + piece * part, part), part),
                        pl.ds(pl.multiple_of(k * hidden + hid_at, width), width)] = value
                else:
                    wd[pl.ds(pl.multiple_of(hid_at + piece * part, part), part), pl.ds(at, width)] = value

    per_step = n_h // steps

    @pl.loop(0, steps)
    def _(s):
        @pl.loop(0, n_f)
        def _(f):
            for j in range(per_step):
                spread(s * per_step + j, f)

        advance(s, 0)

        @pl.when(s == steps // 2 - 1)
        def _():
            first(0, 1)

    all_shared(0, 0)
    span = hidden // steps

    def before(g, n):
        at = pl.multiple_of(n * span, span)
        x = tok[g].reshape(group_rows, features)
        gate = jnp.dot(x, wgu[:, pl.ds(at, span)], preferred_element_type=F32)
        up = jnp.dot(x, wgu[:, pl.ds(pl.multiple_of(hidden + at, span), span)], preferred_element_type=F32)
        return gate, up

    def after(g, n, gate, up):
        at = pl.multiple_of(n * span, span)
        back = lax.dot_general(
            cot[g].reshape(group_rows, features), wd[pl.ds(at, span), :], NT, preferred_element_type=F32
        )
        sig = jax.nn.sigmoid(gate)
        silu = gate * sig
        hid[g, :, pl.ds(at, span)] = (silu * up).astype(BF16)
        grads[g, :, pl.ds(at, span)] = (back * up * sig * (1.0 + gate * (1.0 - sig))).astype(BF16)
        grads[g, :, pl.ds(pl.multiple_of(hidden + at, span), span)] = (back * silu).astype(BF16)

    @pl.loop(0, steps)
    def _(s):
        gate, up = before(0, s)
        pre[s, 0] = gate
        pre[s, 1] = up
        advance(s, 1)

    for a in range(4):
        cross(0, a).wait_recv()
    first(1, 0)
    first(1, 1)
    all_shared(0, 1)

    @pl.loop(0, steps)
    def _(s):
        after(0, s, pre[s, 0], pre[s, 1])

    crossed(2)
    crossed(chips - 2)

    chunk = half // CHUNKS
    chip_rows = group_rows // chips

    def terms(at):
        return lax.dot_general(grads[0], wgu[pl.ds(at, chunk), :], NT, preferred_element_type=F32)

    def to_sibling(i):
        return pltpu.make_async_remote_copy(
            src_ref=sib_out.at[i], dst_ref=sib_in.at[i], send_sem=half_send.at[i], recv_sem=half_recv.at[i],
            device_id=(dp, sibling), device_id_type=MESH,
        )

    def spread_sum(r, i):
        other = (chip + r) % chips
        return pltpu.make_async_remote_copy(
            src_ref=chip_sum.at[i, other], dst_ref=a2a.at[i, r],
            send_sem=a2a_send.at[i, r], recv_sem=a2a_recv.at[i, r],
            device_id=(dp, other * 2 + core), device_id_type=MESH,
        )

    def pair_sum(i):
        to_sibling(i).wait_recv()

        @pl.loop(0, chips)
        def _(c):
            at = pl.ds(pl.multiple_of(c * chip_rows, chip_rows), chip_rows)
            total = acc[i, at, :] + sib_in[i, at, :].astype(F32)
            acc[i, at, :] = total
            chip_sum[i, c] = total.astype(BF16)

        @pl.loop(1, chips)
        def _(r):
            spread_sum(r, i).start()

    @pl.loop(0, CHUNKS)
    def _(i):
        at = pl.multiple_of(i * chunk, chunk)
        sib_out[i] = terms(pl.multiple_of((1 - core) * half + at, chunk)).astype(BF16)
        to_sibling(i).start()
        acc[i] = terms(pl.multiple_of(core * half + at, chunk))

        @pl.when(i > 0)
        def _():
            pair_sum(i - 1)

    pair_sum(CHUNKS - 1)

    for direction in range(2):
        for a in range(4):
            ring_arrival(1, direction, 0, a).wait_recv()
            share(1, 1 if direction == 0 else chips - 1, a).start()

    @pl.loop(3, chips - 2)
    def _(k):
        crossed(k)

    all_shared(1, 0)
    all_shared(1, 1)

    @pl.loop(0, steps)
    def _(s):
        gate, up = before(1, s)
        after(1, s, gate, up)

    def take_part(block):
        out = block[:part]
        for i in range(1, width // part):
            out = jnp.where(dp == i, block[i * part:(i + 1) * part], out)
        return out

    for g in range(2):
        for h in range(n_h):
            hid_t[pl.ds(h * part, part), pl.ds(g * group_rows, group_rows)] = take_part(
                hid[g, :, pl.ds(h * width, width)].T
            )
    four = 4

    @pl.loop(0, n_f // four)
    def _(i):
        at = pl.multiple_of(i * four * width, four * width)
        for g in range(2):
            for b in range(four):
                piece = tok[g, :, :, pl.ds(pl.multiple_of(at + b * width, width), width)]
                lhs[pl.ds(b * part, part), pl.ds(g * group_rows, group_rows)] = take_part(
                    piece.reshape(group_rows, width).T
                )
        for n in range(2 * n_h // 4):
            cut = slice(n * 4 * width, (n + 1) * 4 * width)
            out = jnp.dot(
                lhs[...], grads[:, :, cut].reshape(2 * group_rows, 4 * width), preferred_element_type=F32
            ).astype(BF16)
            for h in range(4):
                for b in range(four):
                    blocks[(n * 4 + h) * n_f + i * four + b] = out[
                        b * part:(b + 1) * part, h * width:(h + 1) * width
                    ]
        c = cot[:, :, :, pl.ds(at, four * width)].reshape(2 * group_rows, four * width)
        out = jnp.dot(hid_t[...], c, preferred_element_type=F32).astype(BF16)
        for h in range(n_h):
            for b in range(four):
                blocks[(2 * n_h + h) * n_f + i * four + b] = out[
                    h * part:(h + 1) * part, b * width:(b + 1) * width
                ]

    @pl.loop(0, wg_ref.shape[0], unroll=8)
    def _(s):
        wg_ref[s] = blocks[slots_ref[s]]

    mine = pl.ds(pl.multiple_of(chip * chip_rows, chip_rows), chip_rows)

    @pl.loop(0, CHUNKS)
    def _(i):
        total = acc[i, mine, :]
        for r in range(1, chips):
            spread_sum(r, i).wait_recv()
            total = total + a2a[i, r].astype(F32)
        low, high = total[:rows], total[rows:]
        at = pl.multiple_of(i * chunk, chunk)
        fin_out[:, pl.ds(at, chunk)] = jnp.where(core == 0, high, low)
        in_ref[:, pl.ds(pl.multiple_of(core * half + at, chunk), chunk)] = jnp.where(core == 0, low, high)

    fin = pltpu.make_async_remote_copy(
        src_ref=fin_out, dst_ref=fin_in, send_sem=fin_send, recv_sem=fin_recv,
        device_id=(dp, sibling), device_id_type=MESH,
    )
    fin.start()

    @pl.loop(0, CHUNKS)
    def _(i):
        to_sibling(i).wait_send()

        @pl.loop(1, chips)
        def _(r):
            spread_sum(r, i).wait_send()

    for a in range(4):
        @pl.loop(0, chips)
        def _(k):
            share(0, k, a).wait_send()
            share(1, k, a).wait_send()

        cross(0, a).wait_send()

        @pl.loop(2, chips - 1)
        def _(k):
            cross(k, a).wait_send()

        for direction in range(2):
            @pl.loop(0, steps if a % 2 == direction else steps - 1)
            def _(s):
                ring(0, direction, s, a).wait_send()

            ring(1, direction, 0, a).wait_send()

    fin.wait()
    in_ref[:, pl.ds(pl.multiple_of((1 - core) * half, half), half)] = fin_in[...]


def kernel_shards(n_cols, tokens, cotangent, block_weights, slot_block, slot_target, counts):
    n_slots, width = block_weights.shape[:2]
    n_dp = 2
    part = width // n_dp
    rows, features = tokens.shape
    n_f = features // width
    hidden_blocks = n_slots // SPC
    hidden = hidden_blocks * width
    places = 3 * hidden_blocks * n_f
    place = slot_target * n_f + slot_block
    number = jnp.arange(n_slots, dtype=jnp.int32)
    live = number < counts[0]
    hit = (place[None, :] == jnp.arange(places, dtype=jnp.int32)[:, None]) & live[None, :]
    table = places + jnp.sum(jnp.where(hit, number[None, :] - places, 0), axis=1)
    slots = jnp.where(live, place, 0)
    chips = n_cols // 2
    group_rows = rows * n_cols
    half = features // 2
    dma = pltpu.SemaphoreType.DMA
    vmem = pl.BlockSpec(memory_space=pltpu.VMEM)
    smem = pl.BlockSpec(memory_space=pltpu.SMEM)
    input_sum, weight_sum = pl.pallas_call(
        functools.partial(layer_kernel, n_cols),
        out_shape=(
            jax.ShapeDtypeStruct((rows, features), F32),
            jax.ShapeDtypeStruct((n_slots, part, width), BF16),
        ),
        in_specs=[smem, smem, vmem, vmem, pl.BlockSpec(memory_space=pl.ANY)],
        out_specs=(vmem, vmem),
        scratch_shapes=[
            pltpu.VMEM((n_dp, n_cols, rows, features), BF16),
            pltpu.VMEM((n_dp, n_cols, rows, features), BF16),
            pltpu.VMEM((places + 1, part, width), BF16),
            pltpu.VMEM((features, 2 * hidden), BF16),
            pltpu.VMEM((hidden, features), BF16),
            pltpu.VMEM((n_dp, group_rows, 2 * hidden), BF16),
            pltpu.VMEM((n_dp, group_rows, hidden), BF16),
            pltpu.VMEM((chips // 2, 2, group_rows, hidden // (chips // 2)), F32),
            pltpu.VMEM((CHUNKS, group_rows, half // CHUNKS), F32),
            pltpu.VMEM((CHUNKS, group_rows, half // CHUNKS), BF16),
            pltpu.VMEM((CHUNKS, group_rows, half // CHUNKS), BF16),
            pltpu.VMEM((CHUNKS, chips, group_rows // chips, half // CHUNKS), BF16),
            pltpu.VMEM((CHUNKS, chips, group_rows // chips, half // CHUNKS), BF16),
            pltpu.VMEM((rows, half), F32),
            pltpu.VMEM((rows, half), F32),
            pltpu.VMEM((4 * part, n_dp * group_rows), BF16),
            pltpu.VMEM((hidden // n_dp, n_dp * group_rows), BF16),
            dma, dma((2,)),
            dma((2, 2, chips // 2, 4)), dma((2, 2, chips // 2, 4)),
            dma((2, chips, 4)), dma((2, chips, 4)),
            dma((chips, 4)), dma((chips, 4)), dma((CHUNKS,)), dma((CHUNKS,)),
            dma((CHUNKS, chips)), dma((CHUNKS, chips)), dma, dma,
        ],
        compiler_params=pltpu.CompilerParams(
            collective_id=0, has_side_effects=True, vmem_limit_bytes=67043328
        ),
    )(table, slots, tokens, cotangent, block_weights.reshape(n_slots * n_dp, part, width))
    weight_grad = jnp.where(live[:, None, None], weight_sum, jnp.zeros((), BF16))
    return (input_sum.astype(BF16), weight_grad)


def solution(mesh):
    n_dp, n_cols = mesh.shape["dp"], mesh.shape["cols"]
    paired = n_dp == 2 and n_cols % 4 == 0

    def body(*args):
        tokens, weights = args[0], args[2]
        if paired and tokens.shape[0] % 16 == 0 and weights.shape[0] // SPC % (n_cols // 4) == 0:
            return kernel_shards(n_cols, *args)
        return shards(*args)

    return jax.shard_map(
        body,
        mesh=mesh,
        in_specs=(
            P(("dp", "cols"), None),
            P(("dp", "cols"), None),
            P("cols", None, None),
            P("cols"),
            P("cols"),
            P("cols"),
        ),
        out_specs=(P(("dp", "cols"), None), P("cols", "dp", None)),
        check_vma=False,
    )
```
